32 devices in a mesh: row: 8 (over y, x, core), col: 4 (over z).
Axes of the slice: x: 2, y: 2, z: 4, core: 2. Of those that a mesh axis runs over, the one named last changes fastest.
Arguments:
- features_t: float32 [18432, 512], P(('row', 'col')), may hold values from -0.0234375 to 0.0234375
- labels: int32 [512], replicated, may hold values from 0 to 1023
- inv_corr: float32 [18432, 18432], P('row', 'col'), may hold values from -1 to 13, as said below
- heads: float32 [18432, 1024], P('row', 'col'), may hold values from -6 to 6
Outputs:
- inv_corr_new: float32 [18432, 18432], P('row', 'col')
- heads_new: float32 [18432, 1024], P('row', 'col')
The draws below stay inside these ranges and needn't reach their ends.
Inputs may be any that keep to these rules, and one draw needn't show every extreme that they name: inv_corr is symmetric and positive definite, with smallest eigenvalue above 0.5.
All inputs are finite; a program needn't handle non-finite values.
Results may differ from the reference program's by a relative error of at most 0.0001.
Values sent between devices are 32-bit elements; how exact they have to be, the bound alone decides.
No kernel may reach another device: no remote copies, remote signals or barrier semaphores. Data moves between devices by JAX's collectives and lax.ppermute only.
A program may use at most 192 MiB of HBM per device.

```python
import math
import jax
import jax.numpy as jnp
from jax import lax

D = 18432
CLASSES = 1024
EXAMPLES = 256
PHASES = 2
ALL_EXAMPLES = 512


def draw_inv_corr(key, part):
    base = jax.random.fold_in(key, 11)
    diag_key, noise_key = jax.random.split(base)
    diagonal = jax.random.uniform(diag_key, (D,), jnp.float32, 2.0, 6.0)
    noise = jax.random.uniform(noise_key, (D, D), jnp.float32, -1.0, 1.0)
    symmetric = (noise + noise.T) * (0.4 / math.sqrt(D))
    return symmetric + jnp.diag(diagonal)


def with_ends(drawn, key, least, top_value):
    longest = drawn.shape.index(max(drawn.shape))
    spots = []
    for shift in (0, 1):
        where = [jax.random.randint(jax.random.fold_in(key, axis), (), 0, length) for axis, length in enumerate(drawn.shape)]
        where[longest] = (where[longest] + shift) % drawn.shape[longest]
        spots.append(tuple(where))
    return drawn.at[spots[0]].set(least).at[spots[1]].set(top_value)


def level_of(own_key, shape, cuts, least, high):
    level = 1.0
    for axis_at, blocks in cuts:
        steps = jax.random.uniform(jax.random.fold_in(jax.random.fold_in(own_key, 6), axis_at), (blocks,), jnp.float32, least / len(cuts), high / len(cuts))
        level = level * jnp.repeat(jnp.exp(steps), shape[axis_at] // blocks).reshape((-1,) + (1,) * (len(shape) - 1 - axis_at))
    return level


def scatter_about(own_key, extent, spread, bound, cuts=(), kind=jnp.bfloat16):
    result = jax.random.normal(own_key, extent, jnp.float32) * spread
    if len(cuts) > 0:
        result = level_of(own_key, extent, cuts, -0.22, 0.18) * result
    return jnp.clip(result, min=-bound, max=bound).astype(kind)


def setup_inputs(seed: int = 0) -> dict:
    arg_keys = jax.random.split(jax.random.key(seed), 5)
    return {
        "features_t": scatter_about(arg_keys[0], (D, ALL_EXAMPLES), (4 * D) ** -0.5, 0.0234375, ((0, 32),), jnp.float32),
        "labels": with_ends(jax.random.randint(arg_keys[1], (ALL_EXAMPLES,), 0, CLASSES), jax.random.fold_in(arg_keys[1], 1), 0, CLASSES - 1).astype(jnp.int32),
        "inv_corr": draw_inv_corr(jax.random.fold_in(arg_keys[4], 71), 0),
        "heads": scatter_about(arg_keys[3], (D, CLASSES), 1.0, 6.0, ((0, 8), (1, 4)), jnp.float32),
    }


def matmul(left, right):
    return jnp.dot(left.astype(jnp.float32), right.astype(jnp.float32), precision=lax.Precision.HIGHEST, preferred_element_type=jnp.float32)

def contract_rows(left, right):
    return lax.dot_general(left.astype(jnp.float32), right.astype(jnp.float32), (((0,), (0,)), ((), ())), precision=lax.Precision.HIGHEST, preferred_element_type=jnp.float32)

def contract_cols(left, right):
    return lax.dot_general(left.astype(jnp.float32), right.astype(jnp.float32), (((1,), (1,)), ((), ())), precision=lax.Precision.HIGHEST, preferred_element_type=jnp.float32)

def invert_system(gram):
    identity_mat = jnp.eye(gram.shape[0], dtype=jnp.float32)
    factor = jnp.linalg.cholesky(identity_mat + gram)
    return jax.scipy.linalg.cho_solve((factor, True), identity_mat)

def reference(features_t, labels, inv_corr, heads):
    classes = jnp.arange(CLASSES, dtype=jnp.int32)
    targets = (labels[:, None] == classes[None, :]).astype(jnp.float32)
    tile = inv_corr
    head = heads
    for phase in range(PHASES):
        lower = phase * EXAMPLES
        current = features_t[:, lower:lower + EXAMPLES]
        panel = matmul(tile, current)
        gram = contract_rows(current, panel)
        fitted = contract_rows(current, head)
        inverse = invert_system(gram)
        gain = matmul(panel, inverse)
        head = head + matmul(gain, targets[lower:lower + EXAMPLES] - fitted)
        tile = tile - contract_cols(gain, panel)
    return (tile, head)
```

```python
import math

import jax
import jax.numpy as jnp
from jax import lax
from jax.experimental import pallas as pl
from jax.experimental.pallas import tpu as pltpu
from jax.sharding import PartitionSpec as P

BLOCK = 128
LANES = 128
VMEM = 60 * 1024 * 1024
GROUP = 8
BIG = lax.Precision.HIGH
SMALL = lax.Precision.HIGHEST


def product(left, right, dims, precision):
    return lax.dot_general(left, right, (dims, ((), ())), precision=precision, preferred_element_type=jnp.float32)


def matmul(left, right, precision=SMALL):
    return product(left, right, ((1,), (0,)), precision)


def contract_rows(left, right, precision=SMALL):
    return product(left, right, ((0,), (0,)), precision)


def contract_cols(left, right, precision=SMALL):
    return product(left, right, ((1,), (1,)), precision)


def pick(blocks, index):
    return lax.dynamic_index_in_dim(blocks, index, 0, keepdims=False)


def put(blocks, value, index):
    return lax.dynamic_update_index_in_dim(blocks, value, index, 0)


class Places:
    def __init__(self):
        self.rows = lax.axis_size("row")
        self.cols = lax.axis_size("col")
        self.ratio = self.rows // self.cols
        self.row = lax.axis_index("row")
        self.col = lax.axis_index("col")
        self.chip = self.row // self.ratio
        self.core = self.row % self.ratio
        order = []
        for low in range(self.cols // 2):
            order += [low, self.cols - 1 - low]
        self.order = order
        self.where = [order.index(mask) for mask in range(self.cols)]

    def slot_of(self, col):
        return jnp.asarray(self.where, jnp.int32)[col ^ self.chip]


def flip(value, mask, axis, size):
    return lax.ppermute(value, axis, [(i, i ^ mask) for i in range(size)])


def line_step(above, below, step, at):
    above = lax.ppermute(above, "col", [(i, i - 1) for i in range(1, at.cols - step + 1)])
    below = lax.ppermute(below, "col", [(i, i + 1) for i in range(step - 1, at.cols - 1)])
    return above, below


def split_bits(size):
    bits = []
    mask = 1
    while mask < size:
        bits.append(mask)
        mask *= 2
    return bits


def halve(blocks, bits, index, axis, size, scale=1):
    count = len(bits)
    dims = list(reversed(split_bits(blocks.shape[0])))
    value = blocks.reshape((2,) * count + blocks.shape[1:])
    for bit in bits:
        dim = dims.index(bit)
        dims.remove(bit)
        on = (index // bit) % 2
        keep = lax.dynamic_index_in_dim(value, on, dim, keepdims=False)
        away = lax.dynamic_index_in_dim(value, 1 - on, dim, keepdims=False)
        value = keep + flip(away, bit * scale, axis, size)
    return value


def double(own, bits, index, axis, size, scale=1):
    value, dims = own, []
    for bit in reversed(bits):
        other = flip(value, bit * scale, axis, size)
        at_dim = len([d for d in dims if d > bit])
        dims.append(bit)
        on = (index // bit) % 2
        low = jnp.where(on == 0, value, other)
        high = jnp.where(on == 0, other, value)
        value = jnp.stack([low, high], at_dim)
    return value.reshape((2 ** len(bits),) + own.shape)


def plane_scatter(partial, at):
    mine = partial[0]
    for step in range(1, at.ratio):
        mine = mine + flip(partial[step], step, "row", at.rows)
    bits = split_bits(at.cols)
    part = mine.shape[1] // 2
    top = halve(mine[:, :part], bits, at.chip, "row", at.rows, at.ratio)
    low = halve(mine[:, part:], bits[::-1], at.chip, "row", at.rows, at.ratio)
    return jnp.concatenate([top, low], 0)


def plane_gather(own, at):
    bits = split_bits(at.cols)
    part = own.shape[0] // 2
    top = double(own[:part], bits, at.chip, "row", at.rows, at.ratio)
    low = double(own[part:], bits[::-1], at.chip, "row", at.rows, at.ratio)
    mine = jnp.concatenate([top, low], 1)
    return [mine] + [flip(mine, step, "row", at.rows) for step in range(1, at.ratio)]


def to_line(own, at):
    pairs = []
    for row in range(at.rows):
        for col in range(at.cols):
            target = (at.ratio * col + row // at.cols, at.order[row % at.cols] ^ col)
            pairs.append((row * at.cols + col, target[0] * at.cols + target[1]))
    return lax.ppermute(own, ("row", "col"), pairs)


def sum_to_line(value, at):
    return halve(value.reshape(at.rows, -1, value.shape[1]), split_bits(at.rows), at.row, "row", at.rows)


def sum_from_line(piece, at):
    for bit in split_bits(at.cols):
        piece = piece + flip(piece, bit, "col", at.cols)
    return double(piece, split_bits(at.rows), at.row, "row", at.rows).reshape(-1, piece.shape[1])


def sweep_small(work, flipped):
    size = work.shape[0]
    lanes = lax.broadcasted_iota(jnp.int32, (GROUP, size), 1)
    subs = lax.broadcasted_iota(jnp.int32, (GROUP, size), 0)
    all_lanes = lax.broadcasted_iota(jnp.int32, (size, size), 1)

    def body(group, _):
        first = pl.multiple_of(group * GROUP, GROUP)
        rows = work[pl.ds(first, GROUP), :]
        turned = rows.T
        flipped[...] = turned
        corner = flipped[pl.ds(first, GROUP), :]
        b = {}
        for i in range(GROUP):
            for j in range(i, GROUP):
                b[i, j] = jnp.broadcast_to(corner[i : i + 1, j : j + 1], (GROUP, size))
        get = lambda i, j: b[min(i, j), max(i, j)]
        for k in range(GROUP):
            inv = 1.0 / b[k, k]
            scaled = {j: get(k, j) * inv for j in range(GROUP) if j != k}
            for i in range(GROUP):
                for j in range(i, GROUP):
                    if i != k and j != k:
                        b[i, j] = b[i, j] - get(i, k) * scaled[j]
            for j in range(GROUP):
                if j != k:
                    b[min(k, j), max(k, j)] = scaled[j]
            b[k, k] = -inv
        panel = jnp.zeros((GROUP, size), jnp.float32)
        columns = []
        for j in range(GROUP):
            column = get(0, j)
            for i in range(1, GROUP):
                column = jnp.where(subs == i, get(i, j), column)
            columns.append(column)
            panel = panel - column * rows[j : j + 1, :]
        for j in range(GROUP):
            panel = jnp.where(lanes == first + j, columns[j], panel)
        inside = (all_lanes >= first) & (all_lanes < first + GROUP)
        whole = jnp.where(inside, 0.0, work[...])
        for j in range(GROUP):
            whole = whole - turned[:, j : j + 1] * panel[j : j + 1, :]
        work[...] = whole
        work[pl.ds(first, GROUP), :] = panel
        return 0

    lax.fori_loop(0, size // GROUP, body, 0)


def sweep_kernel(which, last, in_ref, out_ref, work, flipped):
    size = work.shape[0]
    here = slice(which * size, (which + 1) * size)
    work[...] = in_ref[here, here]
    sweep_small(work, flipped)
    corner = work[...]
    dot = lambda x, y: jnp.dot(x, y, precision=lax.Precision.HIGHEST, preferred_element_type=jnp.float32)
    panel = -dot(corner, in_ref[here, :])
    lanes = lax.broadcasted_iota(jnp.int32, panel.shape, 1)
    inside = (lanes >= which * size) & (lanes < (which + 1) * size)
    wide = jnp.concatenate([corner] * (panel.shape[1] // size), 1)
    panel = jnp.where(inside, wide, panel)
    sign = -1.0 if last else 1.0
    for block in range(in_ref.shape[0] // size):
        there = slice(block * size, (block + 1) * size)
        if block == which:
            out_ref[there, :] = panel * sign
        else:
            rows = in_ref[there, :]
            out_ref[there, :] = (jnp.where(inside, 0.0, rows) - dot(rows[:, here], panel)) * sign


def invert(matrix):
    order = matrix.shape[0]
    count = order // BLOCK
    for which in range(count):
        matrix = pl.pallas_call(
            lambda *refs, which=which: sweep_kernel(which, which == count - 1, *refs),
            out_shape=jax.ShapeDtypeStruct((order, order), jnp.float32),
            in_specs=[pl.BlockSpec(memory_space=pltpu.VMEM)],
            out_specs=pl.BlockSpec(memory_space=pltpu.VMEM),
            scratch_shapes=[pltpu.VMEM((BLOCK, BLOCK), jnp.float32), pltpu.VMEM((BLOCK, GROUP), jnp.float32)],
            compiler_params=pltpu.CompilerParams(vmem_limit_bytes=16 * 1024 * 1024),
            cost_estimate=pl.CostEstimate(flops=10_000_000_000, bytes_accessed=2 * 4 * order * order, transcendentals=0),
            name=f"sweep_{which}",
        )(matrix)
    return matrix


def split(value):
    high = value.astype(jnp.bfloat16)
    return high, (value - high.astype(jnp.float32)).astype(jnp.bfloat16)


def three_products(left, right, dims):
    dot = lambda x, y: lax.dot_general(x, y, (dims, ((), ())), preferred_element_type=jnp.float32)
    return dot(left[0], right[1]) + dot(left[1], right[0]) + dot(left[0], right[0])


def product_kernel(more, last, where_ref, block_ref, tile_ref, *refs):
    out_refs, (high_ref, low_ref) = refs[more:-2], refs[-2:]

    @pl.when(pl.program_id(0) == 0)
    def _():
        high_ref[...], low_ref[...] = split(block_ref[...].T)

    value = three_products((high_ref[...], low_ref[...]), split(tile_ref[...]), ((1,), (0,)))
    if more:
        value = value + refs[0][...]
    if not last:
        out_refs[0][...] = value
        return
    turned = value.T
    cores = len(out_refs)
    chips, height = out_refs[0].shape[:2]
    for chip in range(chips):
        rows = [turned[(chip * cores + core) * height : (chip * cores + core + 1) * height] for core in range(cores)]
        for away in range(cores):
            out_refs[away][chip] = choose(rows, where_ref[1] ^ away)


def choose(values, index):
    value = values[0]
    for number in range(1, len(values)):
        value = jnp.where(index == number, values[number], value)
    return value


def product_step(block, tile, before, place, at, last):
    height, examples = block.shape
    chips = LANES // math.gcd(at.ratio * height, LANES)
    width = at.ratio * height * chips
    more = before is not None
    wide = pl.BlockSpec((examples, width), lambda i, s: (0, i))
    if last:
        out_spec = [pl.BlockSpec((chips, height, examples), lambda i, s: (i, 0, 0))] * at.ratio
        out_shape = [jax.ShapeDtypeStruct((at.cols, height, examples), jnp.float32)] * at.ratio
    else:
        out_spec, out_shape = wide, jax.ShapeDtypeStruct((examples, tile.shape[1]), jnp.float32)
    return pl.pallas_call(
        lambda *refs: product_kernel(more, last, *refs),
        grid_spec=pltpu.PrefetchScalarGridSpec(
            num_scalar_prefetch=1,
            grid=(at.cols // chips,),
            in_specs=[pl.BlockSpec((height, examples), lambda i, s: (0, 0)), pl.BlockSpec((height, width), lambda i, s: (s[0], i))]
            + [wide] * more,
            out_specs=out_spec,
            scratch_shapes=[pltpu.VMEM((examples, height), jnp.bfloat16)] * 2,
        ),
        out_shape=out_shape,
        compiler_params=pltpu.CompilerParams(vmem_limit_bytes=VMEM),
        cost_estimate=pl.CostEstimate(flops=6 * height * examples * tile.shape[1], bytes_accessed=4 * (height + 2 * examples) * tile.shape[1], transcendentals=0),
        name="product_last" if last else "product",
    )(jnp.stack([place, at.core]).astype(jnp.int32), block, tile, *([before] * more))


def update_kernel(parts, where_ref, gain_ref, tile_ref, *refs):
    part_refs, (out_ref, high_ref, low_ref) = refs[:parts], refs[parts:]

    @pl.when(pl.program_id(1) == 0)
    def _():
        chips, height = part_refs[0].shape[:2]
        for chip in range(chips):
            rows = [ref[chip] for ref in part_refs]
            for core in range(parts):
                first = (chip * parts + core) * height
                high_ref[first : first + height], low_ref[first : first + height] = split(choose(rows, where_ref[0] ^ core))

    out_ref[...] = tile_ref[...] - three_products(split(gain_ref[...]), (high_ref[...], low_ref[...]), ((1,), (1,)))


def update(tile, gain, parts, at):
    height, examples = parts[0].shape[1:]
    chips = LANES // math.gcd(at.ratio * height, LANES)
    width = at.ratio * height * chips
    block = pl.BlockSpec((height, width), lambda i, j, s: (j, i))
    return pl.pallas_call(
        lambda *refs: update_kernel(len(parts), *refs),
        grid_spec=pltpu.PrefetchScalarGridSpec(
            num_scalar_prefetch=1,
            grid=(tile.shape[1] // width, tile.shape[0] // height),
            in_specs=[pl.BlockSpec((height, examples), lambda i, j, s: (j, 0)), block]
            + [pl.BlockSpec((chips, height, examples), lambda i, j, s: (i, 0, 0))] * len(parts),
            out_specs=block,
            scratch_shapes=[pltpu.VMEM((width, examples), jnp.bfloat16)] * 2,
        ),
        out_shape=jax.ShapeDtypeStruct(tile.shape, jnp.float32),
        compiler_params=pltpu.CompilerParams(vmem_limit_bytes=VMEM),
        cost_estimate=pl.CostEstimate(flops=6 * examples * tile.size, bytes_accessed=8 * tile.size, transcendentals=0),
        name="update",
    )(at.core.reshape(1).astype(jnp.int32), gain, tile, *parts)


def gather_and_multiply(features_t, inv_corr, at):
    height, examples = features_t.shape
    count, col = at.cols, at.col

    blocks = put(jnp.zeros((count, height, examples), jnp.float32), features_t, col)
    partial = product_step(features_t, inv_corr, None, col, at, False)
    above, below = [None], [None]
    high, low = features_t, features_t
    for step in range(1, count):
        high, low = line_step(high, low, step, at)
        high, low, partial = lax.optimization_barrier((high, low, partial))
        above.append(high)
        below.append(low)
        early = count - step
        if step < early:
            block = jnp.where(col + step < count, high, low)
            place = jnp.where(col + step < count, col + step, col - step)
        elif step == early:
            block, place = high + low, (col + step) % count
        else:
            block = jnp.where(col + early < count, below[early] + high, low)
            place = jnp.where(col + early < count, (col - early) % count, (col + early) % count)
        partial = product_step(block, inv_corr, partial, place, at, step == count - 1)
        blocks = put(blocks, block, place)
    return blocks.reshape(count * height, examples), partial


def on_device(features_t, labels, inv_corr, heads):
    at = Places()
    height, examples = features_t.shape
    features, partial = gather_and_multiply(features_t, inv_corr, at)
    owned = plane_scatter(partial, at)

    moved = to_line(owned, at)
    slot = at.slot_of(at.col)
    gram = sum_to_line(contract_rows(lax.dynamic_slice_in_dim(features, slot * height, height, 0), moved), at)
    above, below = [None], [None]
    held = moved, moved
    fitted = contract_rows(features, heads, BIG)
    waits = [(bit, min(at.cols - 1, number)) for number, bit in enumerate(split_bits(at.rows))]
    for step in range(1, at.cols):
        held = line_step(*held, step, at)
        for bit, window in waits:
            if window == step - 1:
                fitted = fitted + flip(fitted, bit, "row", at.rows)
        if step == 1:
            held, gram, owned, fitted = lax.optimization_barrier((held, gram, owned, fitted))
            gram = sum_from_line(gram, at)
            col_side = plane_gather(owned, at)
        elif step < at.cols - 1:
            held, gram, fitted = lax.optimization_barrier((held, gram, fitted))
        above.append(held[0])
        below.append(held[1])
    for bit, window in waits:
        if window >= at.cols - 1:
            fitted = fitted + flip(fitted, bit, "row", at.rows)
    blocks = put(jnp.zeros((at.cols, height, examples), jnp.float32), moved, slot)
    for step in range(1, at.cols):
        blocks = put(blocks, above[step] + below[at.cols - step], at.slot_of((at.col + step) % at.cols))
    row_side = blocks.reshape(at.cols * height, examples)

    inverse = invert(gram + jnp.eye(examples, dtype=jnp.float32))
    width = heads.shape[1]
    classes = at.col * width + jnp.arange(width, dtype=jnp.int32)
    targets = (labels[:, None] == classes[None, :]).astype(jnp.float32)
    gain = matmul(row_side, inverse, BIG)
    head = heads + matmul(gain, targets - fitted, BIG)
    tile = update(inv_corr, gain, col_side, at)
    return (tile, head)


def solution(mesh):
    placed = (P(("row", "col"), None), P(), P("row", "col"), P("row", "col"))
    return jax.shard_map(
        on_device,
        mesh=mesh,
        in_specs=placed,
        out_specs=(P("row", "col"), P("row", "col")),
        check_vma=False,
    )
```

```python
import jax
import jax.numpy as jnp
from jax import lax
from jax.experimental import pallas as pl
from jax.experimental.pallas import tpu as pltpu
from jax.sharding import PartitionSpec as P

BLOCK = 128
WIDE = 768
VMEM = 60 * 1024 * 1024
GROUP = 8
BIG = lax.Precision.HIGH
SMALL = lax.Precision.HIGHEST


def product(left, right, dims, precision):
    return lax.dot_general(left, right, (dims, ((), ())), precision=precision, preferred_element_type=jnp.float32)


def matmul(left, right, precision=SMALL):
    return product(left, right, ((1,), (0,)), precision)


def contract_rows(left, right, precision=SMALL):
    return product(left, right, ((0,), (0,)), precision)


def contract_cols(left, right, precision=SMALL):
    return product(left, right, ((1,), (1,)), precision)


def pick(blocks, index):
    return lax.dynamic_index_in_dim(blocks, index, 0, keepdims=False)


def put(blocks, value, index):
    return lax.dynamic_update_index_in_dim(blocks, value, index, 0)


class Places:
    def __init__(self):
        self.rows = lax.axis_size("row")
        self.cols = lax.axis_size("col")
        self.ratio = self.rows // self.cols
        self.row = lax.axis_index("row")
        self.col = lax.axis_index("col")
        self.chip = self.row // self.ratio
        self.core = self.row % self.ratio
        self.piece = self.chip ^ choose([jnp.int32(reverse_bits(col, self.cols)) for col in range(self.cols)], self.col)


def reverse_bits(value, size):
    result, mask = 0, 1
    while mask < size:
        result = 2 * result + value // mask % 2
        mask *= 2
    return result


def choose(values, index):
    value = values[0]
    for number in range(1, len(values)):
        value = jnp.where(index == number, values[number], value)
    return value


def flip(value, mask, axis, size):
    return lax.ppermute(value, axis, [(i, i ^ mask) for i in range(size)])


def line_step(above, below, step, at):
    above = lax.ppermute(above, "col", [(i, i - 1) for i in range(1, at.cols - step + 1)])
    below = lax.ppermute(below, "col", [(i, i + 1) for i in range(step - 1, at.cols - 1)])
    return above, below


def split_bits(size):
    bits = []
    mask = 1
    while mask < size:
        bits.append(mask)
        mask *= 2
    return bits


def halve(blocks, bits, index, axis, size, scale=1):
    count = len(bits)
    dims = list(reversed(split_bits(blocks.shape[0])))
    value = blocks.reshape((2,) * count + blocks.shape[1:])
    for bit in bits:
        dim = dims.index(bit)
        dims.remove(bit)
        on = (index // bit) % 2
        keep = lax.dynamic_index_in_dim(value, on, dim, keepdims=False)
        away = lax.dynamic_index_in_dim(value, 1 - on, dim, keepdims=False)
        value = keep + flip(away, bit * scale, axis, size)
    return value


def double(own, bits, index, axis, size, scale=1):
    value, dims = own, []
    for bit in reversed(bits):
        other = flip(value, bit * scale, axis, size)
        at_dim = len([d for d in dims if d > bit])
        dims.append(bit)
        on = (index // bit) % 2
        low = jnp.where(on == 0, value, other)
        high = jnp.where(on == 0, other, value)
        value = jnp.stack([low, high], at_dim)
    return value.reshape((2 ** len(bits),) + own.shape)


def plane_scatter(mine, at):
    bits = split_bits(at.cols)
    part = mine.shape[1] // 2
    top = halve(mine[:, :part], bits, at.piece, "row", at.rows, at.ratio)
    low = halve(mine[:, part:], bits[::-1], at.piece, "row", at.rows, at.ratio)
    return jnp.concatenate([top, low], 0)


def line_pairs(at):
    for row in range(at.rows):
        for col in range(at.cols):
            chip, core = row // at.ratio, row % at.ratio
            yield (row, col), (at.ratio * col + core, chip ^ reverse_bits(col, at.cols))


def to_line(own, at):
    pairs = [(row * at.cols + col, to_row * at.cols + to_col) for (row, col), (to_row, to_col) in line_pairs(at)]
    return lax.ppermute(own, ("row", "col"), pairs)


def to_plane(own, at):
    within, along = [], []
    for (row, col), (from_row, from_col) in line_pairs(at):
        within.append((from_row * at.cols + from_col, row * at.cols + from_col))
        along.append((row * at.cols + from_col, row * at.cols + col))
    between = lax.ppermute(own, ("row", "col"), within)
    return lambda hold: lax.ppermute(lax.optimization_barrier((between, hold))[0], ("row", "col"), along)


def sum_to_line(value, at):
    return halve(value.reshape(at.rows, -1, value.shape[1]), split_bits(at.rows), at.row, "row", at.rows)


def sum_from_line(piece, at):
    for bit in split_bits(at.cols):
        piece = piece + flip(piece, bit, "col", at.cols)
    return double(piece, split_bits(at.rows), at.row, "row", at.rows).reshape(-1, piece.shape[1])


def sweep_small(work, flipped):
    size = work.shape[0]
    lanes = lax.broadcasted_iota(jnp.int32, (GROUP, size), 1)
    subs = lax.broadcasted_iota(jnp.int32, (GROUP, size), 0)
    all_lanes = lax.broadcasted_iota(jnp.int32, (size, size), 1)

    def body(group, _):
        first = pl.multiple_of(group * GROUP, GROUP)
        rows = work[pl.ds(first, GROUP), :]
        turned = rows.T
        flipped[...] = turned
        corner = flipped[pl.ds(first, GROUP), :]
        b = {}
        for i in range(GROUP):
            for j in range(i, GROUP):
                b[i, j] = jnp.broadcast_to(corner[i : i + 1, j : j + 1], (GROUP, size))
        get = lambda i, j: b[min(i, j), max(i, j)]
        for k in range(GROUP):
            inv = 1.0 / b[k, k]
            scaled = {j: get(k, j) * inv for j in range(GROUP) if j != k}
            for i in range(GROUP):
                for j in range(i, GROUP):
                    if i != k and j != k:
                        b[i, j] = b[i, j] - get(i, k) * scaled[j]
            for j in range(GROUP):
                if j != k:
                    b[min(k, j), max(k, j)] = scaled[j]
            b[k, k] = -inv
        panel = jnp.zeros((GROUP, size), jnp.float32)
        columns = []
        for j in range(GROUP):
            column = get(0, j)
            for i in range(1, GROUP):
                column = jnp.where(subs == i, get(i, j), column)
            columns.append(column)
            panel = panel - column * rows[j : j + 1, :]
        for j in range(GROUP):
            panel = jnp.where(lanes == first + j, columns[j], panel)
        inside = (all_lanes >= first) & (all_lanes < first + GROUP)
        whole = jnp.where(inside, 0.0, work[...])
        for j in range(GROUP):
            whole = whole - turned[:, j : j + 1] * panel[j : j + 1, :]
        work[...] = whole
        work[pl.ds(first, GROUP), :] = panel
        return 0

    lax.fori_loop(0, size // GROUP, body, 0)


def sweep_kernel(which, last, in_ref, out_ref, work, flipped):
    size = work.shape[0]
    here = slice(which * size, (which + 1) * size)
    work[...] = in_ref[here, here]
    sweep_small(work, flipped)
    corner = work[...]
    dot = lambda x, y: jnp.dot(x, y, precision=lax.Precision.HIGHEST, preferred_element_type=jnp.float32)
    panel = -dot(corner, in_ref[here, :])
    lanes = lax.broadcasted_iota(jnp.int32, panel.shape, 1)
    inside = (lanes >= which * size) & (lanes < (which + 1) * size)
    wide = jnp.concatenate([corner] * (panel.shape[1] // size), 1)
    panel = jnp.where(inside, wide, panel)
    sign = -1.0 if last else 1.0
    for block in range(in_ref.shape[0] // size):
        there = slice(block * size, (block + 1) * size)
        if block == which:
            out_ref[there, :] = panel * sign
        else:
            rows = in_ref[there, :]
            out_ref[there, :] = (jnp.where(inside, 0.0, rows) - dot(rows[:, here], panel)) * sign


def invert(matrix):
    order = matrix.shape[0]
    count = order // BLOCK
    for which in range(count):
        matrix = pl.pallas_call(
            lambda *refs, which=which: sweep_kernel(which, which == count - 1, *refs),
            out_shape=jax.ShapeDtypeStruct((order, order), jnp.float32),
            in_specs=[pl.BlockSpec(memory_space=pltpu.VMEM)],
            out_specs=pl.BlockSpec(memory_space=pltpu.VMEM),
            scratch_shapes=[pltpu.VMEM((BLOCK, BLOCK), jnp.float32), pltpu.VMEM((BLOCK, GROUP), jnp.float32)],
            compiler_params=pltpu.CompilerParams(vmem_limit_bytes=16 * 1024 * 1024),
            cost_estimate=pl.CostEstimate(flops=10_000_000_000, bytes_accessed=2 * 4 * order * order, transcendentals=0),
            name=f"sweep_{which}",
        )(matrix)
    return matrix


def split(value):
    high = value.astype(jnp.bfloat16)
    return high, (value - high.astype(jnp.float32)).astype(jnp.bfloat16)


def three_products(left, right, dims):
    dot = lambda x, y: lax.dot_general(x, y, (dims, ((), ())), preferred_element_type=jnp.float32)
    return dot(left[0], right[1]) + dot(left[1], right[0]) + dot(left[0], right[0])


def product_kernel(more, last, where_ref, block_ref, tile_ref, *refs):
    out_ref, left_ref = refs[-2:]

    @pl.when(pl.program_id(0) == 0)
    def _():
        high, low = split(block_ref[...].T)
        left_ref[...] = jnp.concatenate([high, high, low], 1)

    high, low = split(tile_ref[...])
    right = jnp.concatenate([high, low, high], 0)
    value = jnp.dot(left_ref[...], right, preferred_element_type=jnp.float32)
    if more:
        value = value + refs[0][...]
    out_ref[...] = value.T if last else value


def block_width(half):
    return max(width for width in range(BLOCK, WIDE + 1, BLOCK) if half % width == 0)


def product_step(block, tile, before, place, at, core=None):
    height, examples = block.shape
    half = tile.shape[1] // at.ratio
    width = block_width(half)
    more, last = before is not None, core is not None
    steps = (half if last else tile.shape[1]) // width
    first = core * (half // width) if last else 0
    wide = pl.BlockSpec((examples, width), lambda i, s: (0, s[1] + i))
    if last:
        out_spec, out_shape = pl.BlockSpec((width, examples), lambda i, s: (i, 0)), (half, examples)
    else:
        out_spec, out_shape = wide, (examples, tile.shape[1])
    return pl.pallas_call(
        lambda *refs: product_kernel(more, last, *refs),
        grid_spec=pltpu.PrefetchScalarGridSpec(
            num_scalar_prefetch=1,
            grid=(steps,),
            in_specs=[pl.BlockSpec((height, examples), lambda i, s: (0, 0)), pl.BlockSpec((height, width), lambda i, s: (s[0], s[1] + i))]
            + [wide] * more,
            out_specs=out_spec,
            scratch_shapes=[pltpu.VMEM((examples, 3 * height), jnp.bfloat16)],
        ),
        out_shape=jax.ShapeDtypeStruct(out_shape, jnp.float32),
        compiler_params=pltpu.CompilerParams(vmem_limit_bytes=VMEM),
        cost_estimate=pl.CostEstimate(flops=6 * height * examples * steps * width, bytes_accessed=4 * (height + 2 * examples) * steps * width, transcendentals=0),
        name="product_last" if last else "product",
    )(jnp.stack([jnp.int32(place), jnp.int32(first)]), block, tile, *([before] * more))


def update_kernel(parts, steps, where_ref, gain_ref, tile_ref, *refs):
    part_refs, (out_ref, left_ref, right_ref) = refs[:parts], refs[parts:]
    step = pl.program_id(0)

    @pl.when(step == 0)
    def _():
        high, low = split(gain_ref[...])
        left_ref[...] = jnp.concatenate([high, high, low], 1)

    for away in range(parts):

        @pl.when(step // steps == away)
        def _():
            high, low = split(part_refs[away][...])
            right_ref[...] = jnp.concatenate([high, low, high], 1)

    change = lax.dot_general(left_ref[...], right_ref[...], (((1,), (1,)), ((), ())), preferred_element_type=jnp.float32)
    out_ref[...] = tile_ref[...] - change


def update(tile, gain, parts, at):
    half, examples = parts[0].shape
    width = block_width(half)
    steps = half // width
    block = pl.BlockSpec((tile.shape[0], width), lambda i, s: (0, ((i // steps) ^ s[0]) * steps + i % steps))
    part = lambda away: pl.BlockSpec((width, examples), lambda i, s: (jnp.clip(i - away * steps, 0, steps - 1), 0))
    return pl.pallas_call(
        lambda *refs: update_kernel(len(parts), steps, *refs),
        grid_spec=pltpu.PrefetchScalarGridSpec(
            num_scalar_prefetch=1,
            grid=(steps * len(parts),),
            in_specs=[pl.BlockSpec(gain.shape, lambda i, s: (0, 0)), block] + [part(away) for away in range(len(parts))],
            out_specs=block,
            scratch_shapes=[pltpu.VMEM((gain.shape[0], 3 * examples), jnp.bfloat16), pltpu.VMEM((width, 3 * examples), jnp.bfloat16)],
        ),
        out_shape=jax.ShapeDtypeStruct(tile.shape, jnp.float32),
        compiler_params=pltpu.CompilerParams(vmem_limit_bytes=VMEM),
        cost_estimate=pl.CostEstimate(flops=6 * examples * tile.size, bytes_accessed=8 * tile.size, transcendentals=0),
        name="update",
    )(at.core.reshape(1).astype(jnp.int32), gain, tile, *parts)


def gather_and_multiply(features_t, inv_corr, at):
    height, examples = features_t.shape
    count, col = at.cols, at.col

    blocks = put(jnp.zeros((count, height, examples), jnp.float32), features_t, col)
    partial = product_step(features_t, inv_corr, None, col, at)
    above, below = [None], [None]
    high, low = features_t, features_t
    for step in range(1, count):
        high, low = line_step(high, low, step, at)
        high, low, partial = lax.optimization_barrier((high, low, partial))
        above.append(high)
        below.append(low)
        early = count - step
        if step < early:
            block = jnp.where(col + step < count, high, low)
            place = jnp.where(col + step < count, col + step, col - step)
        elif step == early:
            block, place = high + low, (col + step) % count
        else:
            block = jnp.where(col + early < count, below[early] + high, low)
            place = jnp.where(col + early < count, (col - early) % count, (col + early) % count)
        blocks = put(blocks, block, place)
        if step < count - 1:
            partial = product_step(block, inv_corr, partial, place, at)
    mine = None
    for away in reversed(range(at.ratio)):
        rows = product_step(block, inv_corr, partial, place, at, at.core ^ away)
        if away > 0:
            rows = flip(rows, away, "row", at.rows)
        mine = rows if mine is None else mine + rows
    return blocks.reshape(count * height, examples), mine.reshape(count, height, examples)


def on_device(features_t, labels, inv_corr, heads):
    at = Places()
    height, examples = features_t.shape
    own_rows = to_plane(features_t, at)
    features, mine = gather_and_multiply(features_t, inv_corr, at)
    own_rows = own_rows(features)
    fitted = contract_rows(features, heads, BIG)
    owned = plane_scatter(mine, at)
    owned, fitted = lax.optimization_barrier((owned, fitted))

    gram = sum_to_line(contract_rows(own_rows, owned), at)
    moved = to_line(owned, at)
    lines = [line_step(moved, moved, 1, at)]
    gated = lax.optimization_barrier((owned, gram))[0]
    gram = sum_from_line(gram, at)
    part = height // 2
    bits = split_bits(at.cols)
    top = double(gated[:part], bits, at.piece, "row", at.rows, at.ratio)
    low = double(gated[part:], bits[::-1], at.piece, "row", at.rows, at.ratio)
    half = jnp.concatenate([top, low], 1).reshape(at.cols * height, examples)
    col_side = [half] + [flip(half, away, "row", at.rows) for away in range(1, at.ratio)]
    for bit in split_bits(at.rows):
        fitted = fitted + flip(fitted, bit, "row", at.rows)

    for step in range(2, at.cols):
        lines.append(line_step(*lines[-1], step, at))
    blocks = put(jnp.zeros((at.cols, height, examples), jnp.float32), moved, at.col)
    for step in range(1, at.cols):
        blocks = put(blocks, lines[step - 1][0] + lines[at.cols - step - 1][1], (at.col + step) % at.cols)
    row_side = blocks.reshape(at.cols * height, examples)

    inverse = invert(gram + jnp.eye(examples, dtype=jnp.float32))
    width = heads.shape[1]
    classes = at.col * width + jnp.arange(width, dtype=jnp.int32)
    targets = (labels[:, None] == classes[None, :]).astype(jnp.float32)
    gain = matmul(row_side, inverse, BIG)
    tile = update(inv_corr, gain, col_side, at)
    head = heads + matmul(gain, targets - fitted, BIG)
    return (tile, head)


def solution(mesh):
    placed = (P(("row", "col"), None), P(), P("row", "col"), P("row", "col"))
    return jax.shard_map(
        on_device,
        mesh=mesh,
        in_specs=placed,
        out_specs=(P("row", "col"), P("row", "col")),
        check_vma=False,
    )
```
